128 devices in a mesh: rows: 64 (over x, y_hi, z, core), grp: 2 (over y_lo).
Axes of the slice: x: 4, y: 4 (y_hi: 2, y_lo: 2; y = y_hi * 2 + y_lo), z: 4, core: 2. Of those that a mesh axis runs over, the one named last changes fastest.
Arguments:
- snapshots: float32 [524288, 256], P(('rows', 'grp'))
- blocks: bfloat16 [4096, 16, 128, 128], P(('rows', 'grp')), may hold values from -96 to 96
- columns: int32 [4096, 16], P(('rows', 'grp')), may hold values from 0 to 63
Outputs:
- projected: float32 [256, 256], replicated
- scaled_factor: float32 [256, 256], replicated
The draws below stay inside these ranges and needn't reach their ends.
Inputs may be any that keep to these rules, and one draw needn't show every extreme that they name: `columns`: each stored block couples its block row to a block row of the same group of 2 * 32 consecutive block rows.
All inputs are finite; a program needn't handle non-finite values.
Results may differ from the reference program's by a relative error of at most 0.003.
Values may be sent and summed in bfloat16 or wider, within the bound.
No kernel may reach another device: no remote copies, remote signals or barrier semaphores. Data moves between devices by JAX's collectives and lax.ppermute only.
A program may use at most 192 MiB of HBM per device.

```python
import math
import jax
import jax.numpy as jnp
from jax import lax

K = 256
BLK = 128
NNZB = 16
NBLK = 32
ROWS = 524288
NBR = 4096
N_GRP = 2


def draw_snapshots(key, part):
    key_base, key_col, key_row = jax.random.split(key, 3)
    base = jax.random.normal(key_base, (ROWS, K), jnp.float32)
    col_scale = jnp.exp(jax.random.uniform(key_col, (1, K), jnp.float32, 0.0, math.log(10.0)))
    row_scale = jnp.exp(jax.random.uniform(key_row, (ROWS, 1), jnp.float32, 0.0, math.log(10.0)))
    values = base * col_scale * row_scale
    return values


def place_ends(array, stream_key, smallest, high):
    longest = array.shape.index(max(array.shape))
    spots = []
    for shift in (0, 1):
        where = [jax.random.randint(jax.random.fold_in(stream_key, axis), (), 0, length) for axis, length in enumerate(array.shape)]
        where[longest] = (where[longest] + shift) % array.shape[longest]
        spots.append(tuple(where))
    return array.at[spots[0]].set(smallest).at[spots[1]].set(high)


def block_levels(stream_key, dims, pieces, smallest, top_value):
    def one(axis_at, parts):
        heights = jax.random.uniform(jax.random.fold_in(jax.random.fold_in(stream_key, 6), axis_at), (parts,), jnp.float32, smallest / len(pieces), top_value / len(pieces))
        return jnp.repeat(jnp.exp(heights), dims[axis_at] // parts).reshape((-1,) + (1,) * (len(dims) - axis_at - 1))

    factor_of = one(*pieces[0])
    for cut in pieces[1:]:
        factor_of = factor_of * one(*cut)
    return factor_of


def centred(own_key, dims, deviation, most, cuts=(), held_as=jnp.bfloat16):
    loudness = block_levels(own_key, dims, cuts, -0.22, 0.18) if cuts else 1.0
    entries = jax.random.normal(own_key, dims, jnp.float32) * deviation * loudness
    return jnp.minimum(jnp.maximum(entries, -most), most).astype(held_as)


def setup_inputs(seed: int = 0) -> dict:
    splits = jax.random.split(jax.random.key(seed), 4)
    return {
        "snapshots": draw_snapshots(jax.random.fold_in(splits[3], 71), 0),
        "blocks": centred(splits[1], (NBR, NNZB, BLK, BLK), ((ROWS // (BLK * NNZB)) ** 0.5), 96.0, ((0, 128),)),
        "columns": place_ends(jax.random.randint(splits[2], (NBR, NNZB), 0, N_GRP * NBLK), jax.random.fold_in(splits[2], 1), 0, (N_GRP * NBLK) - 1).astype(jnp.int32),
    }


def upper_inverse(factor):
    size = factor.shape[0]
    unit_rows = jnp.eye(size, dtype=factor.dtype)

    def substitute(count, inverse):
        index = (size - 1 - count).astype(jnp.int32)
        frow = lax.dynamic_slice_in_dim(factor, index, 1, 0)
        unit = lax.dynamic_slice_in_dim(unit_rows, index, 1, 0)
        pivot = lax.dynamic_slice(factor, (index, index), (1, 1))
        fresh = (unit - jnp.dot(frow, inverse, precision=lax.Precision.HIGHEST)) / pivot
        return lax.dynamic_update_slice_in_dim(inverse, fresh, index, 0)
    return lax.fori_loop(jnp.int32(0), jnp.int32(size), substitute, jnp.zeros_like(factor))

def reference(snapshots, blocks, columns):
    highest = lax.Precision.HIGHEST
    gram = lax.dot_general(snapshots.astype(jnp.float32), snapshots.astype(jnp.float32), (((0,), (0,)), ((), ())), precision=highest, preferred_element_type=jnp.float32)
    factor = jnp.linalg.cholesky(gram).T
    inverse = upper_inverse(factor)
    basis = jnp.dot(snapshots, inverse, precision=highest)
    basis_half = basis.astype(jnp.bfloat16)
    half_blocks = basis_half.reshape(NBR, BLK, K)
    group_len = N_GRP * NBLK
    base = jnp.arange(NBR, dtype=jnp.int32) // group_len * group_len
    target = (base[:, None] + columns).astype(jnp.int32)
    block_groups = blocks.reshape(NBR // NBLK, NBLK, NNZB, BLK, BLK)
    target_groups = target.reshape(NBR // NBLK, NBLK, NNZB)

    def one_group(pair):
        group_blocks, group_target = pair
        picked = half_blocks[group_target]
        return jnp.einsum('bjrc,bjck->brk', group_blocks.astype(jnp.float32), picked.astype(jnp.float32))
    image = lax.map(one_group, (block_groups, target_groups)).reshape(ROWS, K)
    projected = lax.dot_general(basis.astype(jnp.float32), image.astype(jnp.float32), (((0,), (0,)), ((), ())), precision=highest, preferred_element_type=jnp.float32)
    scaled_factor = factor / math.sqrt(ROWS)
    return (projected, scaled_factor)
```

```python
import functools
import math

import jax
import jax.numpy as jnp
from jax import lax
from jax.experimental import pallas as pl
from jax.experimental.pallas import tpu as pltpu
from jax.sharding import PartitionSpec as P

HIGHEST = lax.Precision.HIGHEST
AXES = ("x", "yh", "z", "core", "yl")
SIDE = ("x", "z", "core")
PANEL = 64
FIRST = 8
RAW = 16
KEPT = 8
ROW_TILE = 512
PAIR = 2
LIGHT = pl.CostEstimate(flops=0, transcendentals=0, bytes_accessed=0)
EARLY_VMEM = 40 << 20
LATE_VMEM = 40 << 20


def tdot(left, right):
    return lax.dot_general(left, right, (((0,), (0,)), ((), ())), preferred_element_type=jnp.float32)


def thirds(value):
    high = value.astype(jnp.bfloat16)
    rest = value - high.astype(jnp.float32)
    mid = rest.astype(jnp.bfloat16)
    low = (rest - mid.astype(jnp.float32)).astype(jnp.bfloat16)
    return high, mid, low


def gram_kernel(x_ref, g_ref, sym_ref, off_ref):
    step = pl.program_id(0)

    @pl.when(step == 0)
    def _():
        sym_ref[...] = jnp.zeros_like(sym_ref)
        off_ref[...] = jnp.zeros_like(off_ref)

    high, mid, low = thirds(x_ref[...])
    both = jnp.concatenate([high, mid], axis=0)
    sym_ref[...] += tdot(both, both)
    off_ref[...] += tdot(jnp.concatenate([high, high], axis=0), jnp.concatenate([mid, low], axis=0))

    @pl.when(step == pl.num_programs(0) - 1)
    def _():
        off = off_ref[...]
        g_ref[...] = sym_ref[...] + (off + off.T)


def local_gram(snapshots):
    rows, width = snapshots.shape
    return pl.pallas_call(
        gram_kernel,
        grid=(rows // ROW_TILE,),
        in_specs=[pl.BlockSpec((ROW_TILE, width), lambda i: (i, 0))],
        out_specs=pl.BlockSpec((width, width), lambda i: (0, 0)),
        out_shape=jax.ShapeDtypeStruct((width, width), jnp.float32),
        scratch_shapes=[pltpu.VMEM((width, width), jnp.float32)] * 2,
        cost_estimate=LIGHT,
        name="local_gram",
    )(snapshots)


def factor_kernel(scale, g_ref, sf_ref, inv_ref, r_ref, l_ref):
    n = g_ref.shape[0]
    sub = lax.broadcasted_iota(jnp.int32, (8, 128), 0)
    lane = lax.broadcasted_iota(jnp.int32, (8, 128), 1)
    r_ref[...] = jnp.zeros_like(r_ref)
    l_ref[...] = jnp.zeros_like(l_ref)
    for r0 in range(0, n, PANEL):
        first = r0 // 128
        keys = [("r", i) for i in range(first, n // 128)] + [("l", i) for i in range(first + 1)]
        depth = -(-r0 // 128) * 128
        left = None
        if depth:
            a = first * 128
            left = r_ref[0:depth, a:a + 128].T[r0 - a:r0 - a + PANEL, :]
        tile = {}
        for key in keys:
            kind, i = key
            if kind == "r":
                part = g_ref[r0:r0 + PANEL, i * 128:(i + 1) * 128]
            else:
                rows = lax.broadcasted_iota(jnp.int32, (PANEL, 128), 0) + r0
                cols = lax.broadcasted_iota(jnp.int32, (PANEL, 128), 1) + i * 128
                part = jnp.where(rows == cols, 1.0, 0.0).astype(jnp.float32)
            if depth:
                right = (r_ref if kind == "r" else l_ref)[0:depth, i * 128:(i + 1) * 128]
                part = part - jnp.dot(left, right, precision=HIGHEST, preferred_element_type=jnp.float32)
            for t in range(PANEL // 8):
                tile[t, key] = part[t * 8:(t + 1) * 8, :]
        pk = ("r", first)
        nt = PANEL // 8
        for tk in range(nt):
            c0 = (r0 + tk * 8) % 128
            cols = {}
            for q in range(8):
                for t in range(tk, nt):
                    cols[t, q] = jnp.broadcast_to(tile[t, pk][:, c0 + q:c0 + q + 1], (8, 128))
            rows = {}
            for q in range(8):
                pivot = jnp.broadcast_to(cols[tk, q][q:q + 1, :], (8, 128))
                recip = 1.0 / pivot
                for key in keys:
                    rows[q, key] = jnp.broadcast_to(tile[tk, key][q:q + 1, :], (8, 128)) * recip
                below = jnp.where(sub > q, cols[tk, q], 0.0)
                if q < 7:
                    for key in keys:
                        tile[tk, key] = tile[tk, key] - below * rows[q, key]
                for p in range(q + 1, 8):
                    coef = jnp.broadcast_to(cols[tk, p][q:q + 1, :], (8, 128)) * recip
                    cols[tk, p] = cols[tk, p] - below * coef
                    for t in range(tk + 1, nt):
                        cols[t, p] = cols[t, p] - cols[t, q] * coef
            for t in range(tk + 1, nt):
                for key in keys:
                    acc = tile[t, key]
                    for q in range(8):
                        acc = acc - cols[t, q] * rows[q, key]
                    tile[t, key] = acc
        for t in range(nt):
            at = sub + (r0 + t * 8 - first * 128)
            diag = jnp.sum(jnp.where(lane == at, tile[t, pk], 0.0), axis=1, keepdims=True)
            scale_rows = jnp.broadcast_to(1.0 / jnp.sqrt(diag), (8, 128))
            for key in keys:
                value = tile[t, key] * scale_rows
                if key == pk:
                    value = jnp.where(lane >= at, value, 0.0)
                (r_ref if key[0] == "r" else l_ref)[r0 + t * 8:r0 + t * 8 + 8, key[1] * 128:(key[1] + 1) * 128] = value
    sf_ref[...] = r_ref[...] * scale
    high, mid, low = thirds(l_ref[...].T)
    for at, part in enumerate([high, mid, low, high, mid, high]):
        inv_ref[at * n:(at + 1) * n, :] = part

def factorize(gram, scale):
    size = gram.shape[0]
    return pl.pallas_call(
        functools.partial(factor_kernel, scale),
        out_shape=[
            jax.ShapeDtypeStruct((size, size), jnp.float32),
            jax.ShapeDtypeStruct((6 * size, size), jnp.bfloat16),
        ],
        in_specs=[pl.BlockSpec(memory_space=pltpu.VMEM)],
        out_specs=[pl.BlockSpec(memory_space=pltpu.VMEM)] * 2,
        scratch_shapes=[pltpu.VMEM((size, size), jnp.float32)] * 2,
        cost_estimate=LIGHT,
        name="factorize",
    )(gram)


def basis_of(value, inverse):
    high, mid, low = thirds(value)
    terms = jnp.concatenate([low, mid, high, mid, high, high], axis=1)
    basis = jnp.dot(terms, inverse, preferred_element_type=jnp.float32)
    half = basis.astype(jnp.bfloat16)
    return half, (basis - half.astype(jnp.float32)).astype(jnp.bfloat16)


def late_basis_kernel(x_ref, inv_ref, send_ref, half_ref, low_ref):
    half, low = basis_of(x_ref[...], inv_ref[...])
    send_ref[...] = half
    half_ref[...] = half
    low_ref[...] = low


def late_basis(snapshots, inverse, start):
    rows, width = snapshots.shape
    first = start // ROW_TILE
    shifted = pl.BlockSpec((ROW_TILE, width), lambda i: (i + first, 0))
    half = jax.ShapeDtypeStruct((rows, width), jnp.bfloat16)
    return pl.pallas_call(
        late_basis_kernel,
        grid=((rows - start) // ROW_TILE,),
        in_specs=[shifted, pl.BlockSpec(inverse.shape, lambda i: (0, 0))],
        out_specs=[pl.BlockSpec((ROW_TILE, width), lambda i: (i, 0)), shifted, shifted],
        out_shape=[jax.ShapeDtypeStruct((rows - start, width), jnp.bfloat16), half, half],
        cost_estimate=LIGHT,
        name="late_basis",
    )(snapshots, inverse)


def early_basis_kernel(ends, x_ref, one_ref, two_ref, inv_ref, _, __, half_ref, low_ref, other_ref):
    step = pl.program_id(0)
    value = jnp.where(step < ends[0], x_ref[...], jnp.where(step < ends[1], one_ref[...], two_ref[...]))
    half, low = basis_of(value, inv_ref[...])

    @pl.when(step < ends[0])
    def _():
        half_ref[...] = half
        low_ref[...] = low

    @pl.when(step >= ends[0])
    def _():
        other_ref[...] = half


def early_basis(snapshots, one, two, inverse, half, low):
    width = snapshots.shape[1]
    own = (one.shape[0] + two.shape[0]) // ROW_TILE
    mid = own + one.shape[0] // ROW_TILE
    spec = lambda index: pl.BlockSpec((ROW_TILE, width), index)
    here = spec(lambda i: (jnp.minimum(i, own - 1), 0))
    return pl.pallas_call(
        functools.partial(early_basis_kernel, (own, mid)),
        grid=(2 * own,),
        in_specs=[
            here,
            spec(lambda i: (jnp.clip(i - own, 0, mid - own - 1), 0)),
            spec(lambda i: (jnp.maximum(i - mid, 0), 0)),
            pl.BlockSpec(inverse.shape, lambda i: (0, 0)),
            pl.BlockSpec(memory_space=pl.ANY),
            pl.BlockSpec(memory_space=pl.ANY),
        ],
        out_specs=[here, here, spec(lambda i: (jnp.maximum(i - own, 0), 0))],
        out_shape=[
            jax.ShapeDtypeStruct(half.shape, half.dtype),
            jax.ShapeDtypeStruct(low.shape, low.dtype),
            jax.ShapeDtypeStruct((own * ROW_TILE, width), half.dtype),
        ],
        input_output_aliases={4: 0, 5: 1},
        cost_estimate=LIGHT,
        name="early_basis",
    )(snapshots, one, two, inverse, half, low)


def load_window(step, out_ref, window_ref, sems, pieces, places):
    @pl.when(step == 0)
    def _():
        copies = [
            pltpu.make_async_copy(piece, window_ref.at[pl.ds(at, piece.shape[0])], sems.at[i])
            for i, (piece, at) in enumerate(zip(pieces, places))
        ]
        for copy in copies:
            copy.start()
        out_ref[...] = jnp.zeros_like(out_ref)
        window_ref[window_ref.shape[0] - 1] = jnp.zeros(window_ref.shape[1:], window_ref.dtype)
        for copy in copies:
            copy.wait()


def row_image(block, spot, stored, window_ref):
    image = jnp.zeros(window_ref.shape[1:], jnp.float32)
    for j in range(0, stored, 2):
        left = jnp.concatenate([block(j), block(j + 1)], axis=1)
        right = jnp.concatenate([window_ref[spot(j)], window_ref[spot(j + 1)]], axis=0)
        image += jnp.dot(left, right, preferred_element_type=jnp.float32)
    return image


def add_terms(out_ref, half, low, image):
    high = image.astype(jnp.bfloat16)
    rest = (image - high.astype(jnp.float32)).astype(jnp.bfloat16)
    width = image.shape[1]
    pair = tdot(half, jnp.concatenate([high, rest], axis=1))
    out_ref[...] += pair[:, :width] + (pair[:, width:] + tdot(low, high))


def early_kernel(places, spot_ref, late_ref, blocks_ref, half_ref, low_ref, *refs):
    pieces, (out_ref, kept_ref, window_ref, sems) = refs[:-4], refs[-4:]
    step = pl.program_id(0)
    load_window(step, out_ref, window_ref, sems, pieces, places)
    images = []
    for row in range(PAIR):
        at = step * PAIR + row
        images.append(
            row_image(lambda j: blocks_ref[row, j], lambda j: spot_ref[at, j], blocks_ref.shape[1], window_ref)
        )
        for r in range(kept_ref.shape[1]):
            kept_ref[row, r] = blocks_ref[row, late_ref[at, r]]
    add_terms(out_ref, half_ref[...], low_ref[...], jnp.concatenate(images, axis=0))


def late_kernel(places, spot_ref, late_ref, fill_ref, kept_ref, half_ref, low_ref, blocks_ref, *refs):
    pieces, (out_ref, window_ref, block_ref, sems, block_sem) = refs[:-5], refs[-5:]
    step = pl.program_id(0)
    load_window(step, out_ref, window_ref, sems, pieces, places)
    size = window_ref.shape[1]
    kept = kept_ref.shape[1]
    images = []
    for row in range(PAIR):
        at = step * PAIR + row
        images.append(
            row_image(lambda j: kept_ref[row, j], lambda j: spot_ref[at, j], kept, window_ref)
        )
    add_terms(out_ref, half_ref[...], low_ref[...], jnp.concatenate(images, axis=0))
    for row in range(PAIR):
        at = step * PAIR + row

        @pl.when(fill_ref[at] > kept)
        def _():
            def more(r, image):
                copy = pltpu.make_async_copy(blocks_ref.at[at, late_ref[at, r]], block_ref, block_sem)
                copy.start()
                copy.wait()
                return image + jnp.dot(
                    block_ref[...], window_ref[spot_ref[at, r]], preferred_element_type=jnp.float32
                )

            zero = jnp.zeros(window_ref.shape[1:], jnp.float32)
            image = lax.fori_loop(kept, fill_ref[at], more, zero)
            span = slice(row * size, (row + 1) * size)
            add_terms(out_ref, half_ref[span, :], low_ref[span, :], image)


def as_blocks(pieces, size):
    return [piece.reshape(piece.shape[0] // size, size, piece.shape[1]) for piece in pieces]


def early_terms(spots, late, blocks, half, low, pieces, places, slots):
    count, stored, size, _ = blocks.shape
    width = half.shape[1]
    return pl.pallas_call(
        functools.partial(early_kernel, places),
        grid_spec=pltpu.PrefetchScalarGridSpec(
            num_scalar_prefetch=2,
            grid=(count // PAIR,),
            in_specs=[
                pl.BlockSpec((PAIR, stored, size, size), lambda i, *_: (i, 0, 0, 0)),
                pl.BlockSpec((PAIR * size, width), lambda i, *_: (i, 0)),
                pl.BlockSpec((PAIR * size, width), lambda i, *_: (i, 0)),
            ]
            + [pl.BlockSpec(memory_space=pl.ANY)] * len(pieces),
            out_specs=[
                pl.BlockSpec((width, width), lambda i, *_: (0, 0)),
                pl.BlockSpec((PAIR, KEPT, size, size), lambda i, *_: (i, 0, 0, 0)),
            ],
            scratch_shapes=[
                pltpu.VMEM((slots + 1, size, width), jnp.bfloat16),
                pltpu.SemaphoreType.DMA((len(pieces),)),
            ],
        ),
        out_shape=[
            jax.ShapeDtypeStruct((width, width), jnp.float32),
            jax.ShapeDtypeStruct((count, KEPT, size, size), blocks.dtype),
        ],
        compiler_params=pltpu.CompilerParams(vmem_limit_bytes=EARLY_VMEM),
        cost_estimate=LIGHT,
        name="early_terms",
    )(spots, late, blocks, half, low, *as_blocks(pieces, size))


def late_terms(spots, late, fill, kept, blocks, half, low, pieces, places, slots):
    count, _, size, _ = blocks.shape
    width = half.shape[1]
    return pl.pallas_call(
        functools.partial(late_kernel, places),
        grid_spec=pltpu.PrefetchScalarGridSpec(
            num_scalar_prefetch=3,
            grid=(count // PAIR,),
            in_specs=[
                pl.BlockSpec((PAIR, KEPT, size, size), lambda i, *_: (i, 0, 0, 0)),
                pl.BlockSpec((PAIR * size, width), lambda i, *_: (i, 0)),
                pl.BlockSpec((PAIR * size, width), lambda i, *_: (i, 0)),
            ]
            + [pl.BlockSpec(memory_space=pl.ANY)] * (1 + len(pieces)),
            out_specs=pl.BlockSpec((width, width), lambda i, *_: (0, 0)),
            scratch_shapes=[
                pltpu.VMEM((slots + 1, size, width), jnp.bfloat16),
                pltpu.VMEM((size, size), blocks.dtype),
                pltpu.SemaphoreType.DMA((len(pieces),)),
                pltpu.SemaphoreType.DMA,
            ],
        ),
        out_shape=jax.ShapeDtypeStruct((width, width), jnp.float32),
        compiler_params=pltpu.CompilerParams(vmem_limit_bytes=LATE_VMEM),
        cost_estimate=LIGHT,
        name="late_terms",
    )(spots, late, fill, kept, half, low, blocks, *as_blocks(pieces, size))


def spread(value, axes):
    devices = lax.axis_size(axes)
    rows, width = value.shape
    copies = jnp.broadcast_to(value[None], (devices, rows, width))
    return lax.all_to_all(copies, axes, 0, 0, tiled=True).reshape(devices * rows, width)


def reduce_share(value, axes):
    devices = lax.axis_size(axes)
    rows, width = value.shape
    parts = lax.all_to_all(value.reshape(devices, rows // devices, width), axes, 0, 0, tiled=True)
    return parts.sum(axis=0)


def total(value):
    return spread(reduce_share(value, AXES), AXES)


def exchange(value, axes, mask):
    return lax.ppermute(value, axes, [(i, i ^ mask) for i in range(lax.axis_size(axes))])


def local(snapshots, blocks, columns):
    rows = snapshots.shape[0]
    size = blocks.shape[2]
    count = rows // size
    first, raw = FIRST * size, RAW * size
    partner_first = exchange(snapshots[:first], "yl", 1)
    share = reduce_share(local_gram(snapshots), SIDE)
    share, partner_first = lax.optimization_barrier((share, partner_first))
    near = [exchange(share, ("yh", "yl"), mask) for mask in (1, 2, 3)]
    share = (share + near[0]) + (near[1] + near[2])
    share, following = lax.optimization_barrier((share, snapshots[first:raw]))
    partner_second = exchange(following, "yl", 1)
    gram = spread(share, SIDE)
    total_rows = rows * lax.axis_size(AXES)
    scaled_factor, inverse = factorize(gram, 1.0 / math.sqrt(total_rows))
    late_half, half, low = late_basis(snapshots, inverse, raw)
    partner_late = exchange(late_half, "yl", 1)
    half, low, early_half = early_basis(snapshots, partner_first, partner_second, inverse, half, low)
    own = columns // count == lax.axis_index("yl")
    spots = columns % count + jnp.where(own, 0, count)
    slots = 2 * count
    is_late = spots >= count + RAW
    order = jnp.arange(columns.shape[1])
    ahead = is_late[:, None, :] & (order[None, None, :] < order[None, :, None])
    rank = jnp.where(is_late, ahead.sum(axis=2), slots)
    chosen = rank[:, None, :] == order[None, :, None]
    late = jnp.where(chosen, order[None, None, :], 0).sum(axis=2)
    fill = is_late.sum(axis=1)
    filled = order[None, :] < fill[:, None]
    late_spots = jnp.where(filled, jnp.where(chosen, spots[:, None, :], 0).sum(axis=2), slots)
    early, kept = early_terms(
        jnp.where(is_late, slots, spots), late, blocks, half, low,
        [half, early_half], [0, count], slots,
    )
    rest = late_terms(
        late_spots, late, fill, kept, blocks, half, low, [partner_late], [count + RAW], slots
    )
    projected = total(early + rest)
    return (projected, scaled_factor)


def solution(mesh):
    sizes = (4, 2, 4, 2, 2)
    fine = jax.sharding.Mesh(mesh.devices.reshape(sizes), AXES)
    return jax.shard_map(
        local,
        mesh=fine,
        in_specs=(
            P(AXES, None),
            P(AXES, None, None, None),
            P(AXES, None),
        ),
        out_specs=(P(), P()),
        check_vma=False,
    )
```

```python
import functools
import math

import jax
import jax.numpy as jnp
from jax import lax
from jax.experimental import pallas as pl
from jax.experimental.pallas import tpu as pltpu
from jax.sharding import PartitionSpec as P

HIGHEST = lax.Precision.HIGHEST
AXES = ("x", "yh", "z", "core", "yl")
SIDE = ("x", "z", "core")
PANEL = 64
FIRST = 8
RAW = 16
GRAM_TILE = 2048
ROW_TILE = 1024
PAIR = 8
LIGHT = pl.CostEstimate(flops=0, transcendentals=0, bytes_accessed=0)
EARLY_VMEM = 56 << 20


def tdot(left, right):
    return lax.dot_general(left, right, (((0,), (0,)), ((), ())), preferred_element_type=jnp.float32)


def thirds(value):
    high = value.astype(jnp.bfloat16)
    rest = value - high.astype(jnp.float32)
    mid = rest.astype(jnp.bfloat16)
    low = (rest - mid.astype(jnp.float32)).astype(jnp.bfloat16)
    return high, mid, low


def gram_kernel(x_ref, g_ref, sym_ref, off_ref):
    step = pl.program_id(0)

    @pl.when(step == 0)
    def _():
        sym_ref[...] = jnp.zeros_like(sym_ref)
        off_ref[...] = jnp.zeros_like(off_ref)

    high, mid, low = thirds(x_ref[...])
    both = jnp.concatenate([high, mid], axis=0)
    sym_ref[...] += tdot(both, both)
    off_ref[...] += tdot(jnp.concatenate([high, high], axis=0), jnp.concatenate([mid, low], axis=0))

    @pl.when(step == pl.num_programs(0) - 1)
    def _():
        off = off_ref[...]
        g_ref[...] = sym_ref[...] + (off + off.T)


def local_gram(snapshots):
    rows, width = snapshots.shape
    return pl.pallas_call(
        gram_kernel,
        grid=(rows // GRAM_TILE,),
        in_specs=[pl.BlockSpec((GRAM_TILE, width), lambda i: (i, 0))],
        out_specs=pl.BlockSpec((width, width), lambda i: (0, 0)),
        out_shape=jax.ShapeDtypeStruct((width, width), jnp.float32),
        scratch_shapes=[pltpu.VMEM((width, width), jnp.float32)] * 2,
        cost_estimate=LIGHT,
        name="local_gram",
    )(snapshots)


def factor_kernel(scale, g_ref, sf_ref, inv_ref, r_ref, l_ref):
    n = g_ref.shape[0]
    sub = lax.broadcasted_iota(jnp.int32, (8, 128), 0)
    lane = lax.broadcasted_iota(jnp.int32, (8, 128), 1)
    r_ref[...] = jnp.zeros_like(r_ref)
    l_ref[...] = jnp.zeros_like(l_ref)
    for r0 in range(0, n, PANEL):
        first = r0 // 128
        keys = [("r", i) for i in range(first, n // 128)] + [("l", i) for i in range(first + 1)]
        depth = -(-r0 // 128) * 128
        left = None
        if depth:
            a = first * 128
            left = r_ref[0:depth, a:a + 128].T[r0 - a:r0 - a + PANEL, :]
        tile = {}
        for key in keys:
            kind, i = key
            if kind == "r":
                part = g_ref[r0:r0 + PANEL, i * 128:(i + 1) * 128]
            else:
                rows = lax.broadcasted_iota(jnp.int32, (PANEL, 128), 0) + r0
                cols = lax.broadcasted_iota(jnp.int32, (PANEL, 128), 1) + i * 128
                part = jnp.where(rows == cols, 1.0, 0.0).astype(jnp.float32)
            if depth:
                right = (r_ref if kind == "r" else l_ref)[0:depth, i * 128:(i + 1) * 128]
                part = part - jnp.dot(left, right, precision=HIGHEST, preferred_element_type=jnp.float32)
            for t in range(PANEL // 8):
                tile[t, key] = part[t * 8:(t + 1) * 8, :]
        pk = ("r", first)
        nt = PANEL // 8
        for tk in range(nt):
            c0 = (r0 + tk * 8) % 128
            cols = {}
            for q in range(8):
                for t in range(tk, nt):
                    cols[t, q] = jnp.broadcast_to(tile[t, pk][:, c0 + q:c0 + q + 1], (8, 128))
            rows = {}
            for q in range(8):
                pivot = jnp.broadcast_to(cols[tk, q][q:q + 1, :], (8, 128))
                recip = 1.0 / pivot
                for key in keys:
                    rows[q, key] = jnp.broadcast_to(tile[tk, key][q:q + 1, :], (8, 128)) * recip
                below = jnp.where(sub > q, cols[tk, q], 0.0)
                if q < 7:
                    for key in keys:
                        tile[tk, key] = tile[tk, key] - below * rows[q, key]
                for p in range(q + 1, 8):
                    coef = jnp.broadcast_to(cols[tk, p][q:q + 1, :], (8, 128)) * recip
                    cols[tk, p] = cols[tk, p] - below * coef
                    for t in range(tk + 1, nt):
                        cols[t, p] = cols[t, p] - cols[t, q] * coef
            for t in range(tk + 1, nt):
                for key in keys:
                    acc = tile[t, key]
                    for q in range(8):
                        acc = acc - cols[t, q] * rows[q, key]
                    tile[t, key] = acc
        for t in range(nt):
            at = sub + (r0 + t * 8 - first * 128)
            diag = jnp.sum(jnp.where(lane == at, tile[t, pk], 0.0), axis=1, keepdims=True)
            scale_rows = jnp.broadcast_to(1.0 / jnp.sqrt(diag), (8, 128))
            for key in keys:
                value = tile[t, key] * scale_rows
                if key == pk:
                    value = jnp.where(lane >= at, value, 0.0)
                (r_ref if key[0] == "r" else l_ref)[r0 + t * 8:r0 + t * 8 + 8, key[1] * 128:(key[1] + 1) * 128] = value
    sf_ref[...] = r_ref[...] * scale
    high, mid, low = thirds(l_ref[...].T)
    for at, part in enumerate([high, mid, low, high, mid, high]):
        inv_ref[at * n:(at + 1) * n, :] = part

def factorize(gram, scale):
    size = gram.shape[0]
    return pl.pallas_call(
        functools.partial(factor_kernel, scale),
        out_shape=[
            jax.ShapeDtypeStruct((size, size), jnp.float32),
            jax.ShapeDtypeStruct((6 * size, size), jnp.bfloat16),
        ],
        in_specs=[pl.BlockSpec(memory_space=pltpu.VMEM)],
        out_specs=[pl.BlockSpec(memory_space=pltpu.VMEM)] * 2,
        scratch_shapes=[pltpu.VMEM((size, size), jnp.float32)] * 2,
        cost_estimate=LIGHT,
        name="factorize",
    )(gram)


def basis_of(value, inverse):
    high, mid, low = thirds(value)
    terms = jnp.concatenate([low, mid, high, mid, high, high], axis=1)
    return jnp.dot(terms, inverse, preferred_element_type=jnp.float32)


def own_basis_kernel(x_ref, inv_ref, *refs):
    half_ref, turned_ref = refs[-2:]
    basis = basis_of(x_ref[...], inv_ref[...])
    half = basis.astype(jnp.bfloat16)
    half_ref[...] = half
    if len(refs) == 3:
        refs[0][...] = half
    turned = basis.T
    high = turned.astype(jnp.bfloat16)
    rest = (turned - high.astype(jnp.float32)).astype(jnp.bfloat16)
    size = turned_ref.shape[2] // 2
    for i in range(turned_ref.shape[0]):
        span = slice(i * size, (i + 1) * size)
        turned_ref[i] = jnp.concatenate([high[:, span], rest[:, span]], axis=1)


def own_basis(snapshots, inverse, start, stop, size, held=None):
    rows, width = snapshots.shape
    tile = math.gcd(math.gcd(start, stop), ROW_TILE)
    first = start // tile
    shifted = pl.BlockSpec((tile, width), lambda i: (i + first, 0))
    half = jax.ShapeDtypeStruct((rows, width), jnp.bfloat16)
    turned = jax.ShapeDtypeStruct((rows // size, width, 2 * size), jnp.bfloat16)
    out_specs = [shifted, pl.BlockSpec((tile // size, width, 2 * size), lambda i: (i + first, 0, 0))]
    out_shape = [half, turned]
    if held is None:
        out_specs = [pl.BlockSpec((tile, width), lambda i: (i, 0))] + out_specs
        out_shape = [jax.ShapeDtypeStruct((stop - start, width), jnp.bfloat16)] + out_shape
    held = held or []
    return pl.pallas_call(
        own_basis_kernel,
        grid=((stop - start) // tile,),
        in_specs=[shifted, pl.BlockSpec(inverse.shape, lambda i: (0, 0))]
        + [pl.BlockSpec(memory_space=pl.ANY)] * len(held),
        out_specs=out_specs,
        out_shape=out_shape,
        input_output_aliases={2 + i: i for i in range(len(held))},
        cost_estimate=LIGHT,
        name="own_basis",
    )(snapshots, inverse, *held)


def other_basis_kernel(switch, one_ref, two_ref, inv_ref, out_ref):
    value = jnp.where(pl.program_id(0) < switch, one_ref[...], two_ref[...])
    out_ref[...] = basis_of(value, inv_ref[...]).astype(jnp.bfloat16)


def other_basis(one, two, inverse):
    width = one.shape[1]
    tile = math.gcd(math.gcd(one.shape[0], two.shape[0]), ROW_TILE)
    switch, steps = one.shape[0] // tile, (one.shape[0] + two.shape[0]) // tile
    return pl.pallas_call(
        functools.partial(other_basis_kernel, switch),
        grid=(steps,),
        in_specs=[
            pl.BlockSpec((tile, width), lambda i: (jnp.minimum(i, switch - 1), 0)),
            pl.BlockSpec((tile, width), lambda i: (jnp.maximum(i - switch, 0), 0)),
            pl.BlockSpec(inverse.shape, lambda i: (0, 0)),
        ],
        out_specs=pl.BlockSpec((tile, width), lambda i: (i, 0)),
        out_shape=jax.ShapeDtypeStruct((steps * tile, width), jnp.bfloat16),
        cost_estimate=LIGHT,
        name="other_basis",
    )(one, two, inverse)


def split_pair(value):
    high = value.astype(jnp.bfloat16)
    rest = (value - high.astype(jnp.float32)).astype(jnp.bfloat16)
    return jnp.concatenate([high, rest], axis=1)


def doubled(half):
    return jnp.concatenate([half, half], axis=0)


def early_kernel(places, spot_ref, blocks_ref, turned_ref, *refs):
    pieces, (out_ref, left_ref, sums_ref, window_ref, sems) = refs[:-5], refs[-5:]
    step = pl.program_id(0)
    size = blocks_ref.shape[2]
    copies = [
        pltpu.make_async_copy(piece, window_ref.at[pl.ds(at, piece.shape[0])], sems.at[i])
        for i, (piece, at) in enumerate(zip(pieces, places))
    ]

    @pl.when(step == 0)
    def _():
        for copy in copies:
            copy.start()
        sums_ref[...] = jnp.zeros_like(sums_ref)

    for row in range(PAIR):
        at = step * PAIR + row
        for j in range(0, blocks_ref.shape[1], 2):
            pair = jnp.concatenate([blocks_ref[row, j], blocks_ref[row, j + 1]], axis=1)
            term = jnp.dot(turned_ref[row], doubled(pair), preferred_element_type=jnp.float32)
            sums_ref[spot_ref[at, j]] += term[:, :size]
            sums_ref[spot_ref[at, j + 1]] += term[:, size:]

    @pl.when(step == pl.num_programs(0) - 1)
    def _():
        for copy in copies:
            copy.wait()
        known = window_ref.shape[0]
        total = jnp.zeros_like(out_ref)
        for c in range(known):
            total += jnp.dot(
                split_pair(sums_ref[c]), doubled(window_ref[c]), preferred_element_type=jnp.float32
            )
        out_ref[...] = total
        for c in range(left_ref.shape[0]):
            left_ref[c] = split_pair(sums_ref[known + c])


def early_terms(spots, blocks, turned, pieces, slots):
    count, stored, size, _ = blocks.shape
    width = turned.shape[1]
    pieces = [piece.reshape(piece.shape[0] // size, size, width) for piece in pieces]
    places = [sum(piece.shape[0] for piece in pieces[:i]) for i in range(len(pieces))]
    known = places[-1] + pieces[-1].shape[0]
    return pl.pallas_call(
        functools.partial(early_kernel, places),
        grid_spec=pltpu.PrefetchScalarGridSpec(
            num_scalar_prefetch=1,
            grid=(count // PAIR,),
            in_specs=[
                pl.BlockSpec((PAIR, stored, size, size), lambda i, *_: (i, 0, 0, 0)),
                pl.BlockSpec((PAIR, width, 2 * size), lambda i, *_: (i, 0, 0)),
            ]
            + [pl.BlockSpec(memory_space=pl.ANY)] * len(pieces),
            out_specs=[
                pl.BlockSpec((width, width), lambda i, *_: (0, 0)),
                pl.BlockSpec((slots - known, width, 2 * size), lambda i, *_: (0, 0, 0)),
            ],
            scratch_shapes=[
                pltpu.VMEM((slots, width, size), jnp.float32),
                pltpu.VMEM((known, size, width), jnp.bfloat16),
                pltpu.SemaphoreType.DMA((len(pieces),)),
            ],
        ),
        out_shape=[
            jax.ShapeDtypeStruct((width, width), jnp.float32),
            jax.ShapeDtypeStruct((slots - known, width, 2 * size), jnp.bfloat16),
        ],
        compiler_params=pltpu.CompilerParams(vmem_limit_bytes=EARLY_VMEM),
        cost_estimate=LIGHT,
        name="early_terms",
    )(spots, blocks, turned, *pieces)


def late_kernel(early_ref, left_ref, half_ref, out_ref):
    total = early_ref[...]
    for c in range(left_ref.shape[0]):
        total += jnp.dot(left_ref[c], doubled(half_ref[c]), preferred_element_type=jnp.float32)
    out_ref[...] = total


def late_terms(early, left, half):
    size = left.shape[2] // 2
    return pl.pallas_call(
        late_kernel,
        in_specs=[pl.BlockSpec(memory_space=pltpu.VMEM)] * 3,
        out_specs=pl.BlockSpec(memory_space=pltpu.VMEM),
        out_shape=jax.ShapeDtypeStruct(early.shape, jnp.float32),
        cost_estimate=LIGHT,
        name="late_terms",
    )(early, left, half.reshape(left.shape[0], size, half.shape[1]))


def spread(value, axes):
    devices = lax.axis_size(axes)
    rows, width = value.shape
    copies = jnp.broadcast_to(value[None], (devices, rows, width))
    return lax.all_to_all(copies, axes, 0, 0, tiled=True).reshape(devices * rows, width)


def reduce_share(value, axes):
    devices = lax.axis_size(axes)
    rows, width = value.shape
    parts = lax.all_to_all(value.reshape(devices, rows // devices, width), axes, 0, 0, tiled=True)
    return parts.sum(axis=0)


def total(value):
    return spread(reduce_share(value, AXES), AXES)


def exchange(value, axes, mask):
    return lax.ppermute(value, axes, [(i, i ^ mask) for i in range(lax.axis_size(axes))])


def local(snapshots, blocks, columns):
    rows = snapshots.shape[0]
    size = blocks.shape[2]
    count = rows // size
    first, raw = FIRST * size, RAW * size
    partner_first = exchange(snapshots[:first], "yl", 1)
    share = reduce_share(local_gram(snapshots), SIDE)
    share, partner_first = lax.optimization_barrier((share, partner_first))
    near = [exchange(share, ("yh", "yl"), mask) for mask in (1, 2, 3)]
    share = (share + near[0]) + (near[1] + near[2])
    share, following = lax.optimization_barrier((share, snapshots[first:raw]))
    partner_second = exchange(following, "yl", 1)
    gram = spread(share, SIDE)
    total_rows = rows * lax.axis_size(AXES)
    scaled_factor, inverse = factorize(gram, 1.0 / math.sqrt(total_rows))
    late_half, half, turned = own_basis(snapshots, inverse, raw, rows, size)
    partner_late = exchange(late_half, "yl", 1)
    half, turned = own_basis(snapshots, inverse, 0, raw, size, [half, turned])
    other_half = other_basis(partner_first, partner_second, inverse)
    own = columns // count == lax.axis_index("yl")
    spots = columns % count + jnp.where(own, 0, count)
    early, left = early_terms(spots, blocks, turned, [half, other_half], 2 * count)
    projected = total(late_terms(early, left, partner_late))
    return (projected, scaled_factor)


def solution(mesh):
    sizes = (4, 2, 4, 2, 2)
    fine = jax.sharding.Mesh(mesh.devices.reshape(sizes), AXES)
    return jax.shard_map(
        local,
        mesh=fine,
        in_specs=(
            P(AXES, None),
            P(AXES, None, None, None),
            P(AXES, None),
        ),
        out_specs=(P(), P()),
        check_vma=False,
    )
```

```python
import functools
import math

import jax
import jax.numpy as jnp
from jax import lax
from jax.experimental import pallas as pl
from jax.experimental.pallas import tpu as pltpu
from jax.sharding import PartitionSpec as P

HIGHEST = lax.Precision.HIGHEST
AXES = ("x", "yh", "z", "core", "yl")
SIDE = ("x", "z", "core")
PANEL = 64
FIRST = 8
RAW = 16
GRAM_TILE = 2048
ROW_TILE = 1024
PAIR = 8
LIGHT = pl.CostEstimate(flops=0, transcendentals=0, bytes_accessed=0)
EARLY_VMEM = 56 << 20
LATE_STEPS = 4


def tdot(left, right):
    return lax.dot_general(left, right, (((0,), (0,)), ((), ())), preferred_element_type=jnp.float32)


def thirds(value):
    high = value.astype(jnp.bfloat16)
    rest = value - high.astype(jnp.float32)
    mid = rest.astype(jnp.bfloat16)
    low = (rest - mid.astype(jnp.float32)).astype(jnp.bfloat16)
    return high, mid, low


def gram_kernel(first, x_ref, g_ref, copy_ref, sym_ref, off_ref):
    step = pl.program_id(0)

    @pl.when(step == 0)
    def _():
        copy_ref[...] = x_ref[first:first + copy_ref.shape[0], :]

    @pl.when(step == 0)
    def _():
        sym_ref[...] = jnp.zeros_like(sym_ref)
        off_ref[...] = jnp.zeros_like(off_ref)

    high, mid, low = thirds(x_ref[...])
    both = jnp.concatenate([high, mid], axis=0)
    sym_ref[...] += tdot(both, both)
    off_ref[...] += tdot(jnp.concatenate([high, high], axis=0), jnp.concatenate([mid, low], axis=0))

    @pl.when(step == pl.num_programs(0) - 1)
    def _():
        off = off_ref[...]
        g_ref[...] = sym_ref[...] + (off + off.T)


def local_gram(snapshots, first, stop):
    rows, width = snapshots.shape
    return pl.pallas_call(
        functools.partial(gram_kernel, first),
        grid=(rows // GRAM_TILE,),
        in_specs=[pl.BlockSpec((GRAM_TILE, width), lambda i: (i, 0))],
        out_specs=[
            pl.BlockSpec((width, width), lambda i: (0, 0)),
            pl.BlockSpec((stop - first, width), lambda i: (0, 0)),
        ],
        out_shape=[
            jax.ShapeDtypeStruct((width, width), jnp.float32),
            jax.ShapeDtypeStruct((stop - first, width), jnp.float32),
        ],
        scratch_shapes=[pltpu.VMEM((width, width), jnp.float32)] * 2,
        cost_estimate=LIGHT,
        name="local_gram",
    )(snapshots)


def factor_kernel(scale, g_ref, sf_ref, inv_ref, r_ref, l_ref):
    n = g_ref.shape[0]
    sub = lax.broadcasted_iota(jnp.int32, (8, 128), 0)
    lane = lax.broadcasted_iota(jnp.int32, (8, 128), 1)
    r_ref[...] = jnp.zeros_like(r_ref)
    l_ref[...] = jnp.zeros_like(l_ref)
    for r0 in range(0, n, PANEL):
        first = r0 // 128
        keys = [("r", i) for i in range(first, n // 128)] + [("l", i) for i in range(first + 1)]
        depth = -(-r0 // 128) * 128
        left = None
        if depth:
            a = first * 128
            left = r_ref[0:depth, a:a + 128].T[r0 - a:r0 - a + PANEL, :]
        tile = {}
        for key in keys:
            kind, i = key
            if kind == "r":
                part = g_ref[r0:r0 + PANEL, i * 128:(i + 1) * 128]
            else:
                rows = lax.broadcasted_iota(jnp.int32, (PANEL, 128), 0) + r0
                cols = lax.broadcasted_iota(jnp.int32, (PANEL, 128), 1) + i * 128
                part = jnp.where(rows == cols, 1.0, 0.0).astype(jnp.float32)
            if depth:
                right = (r_ref if kind == "r" else l_ref)[0:depth, i * 128:(i + 1) * 128]
                part = part - jnp.dot(left, right, precision=HIGHEST, preferred_element_type=jnp.float32)
            for t in range(PANEL // 8):
                tile[t, key] = part[t * 8:(t + 1) * 8, :]
        pk = ("r", first)
        nt = PANEL // 8
        for tk in range(nt):
            c0 = (r0 + tk * 8) % 128
            cols = {}
            for q in range(8):
                for t in range(tk, nt):
                    cols[t, q] = jnp.broadcast_to(tile[t, pk][:, c0 + q:c0 + q + 1], (8, 128))
            rows = {}
            for q in range(8):
                pivot = jnp.broadcast_to(cols[tk, q][q:q + 1, :], (8, 128))
                recip = 1.0 / pivot
                for key in keys:
                    rows[q, key] = jnp.broadcast_to(tile[tk, key][q:q + 1, :], (8, 128)) * recip
                below = jnp.where(sub > q, cols[tk, q], 0.0)
                if q < 7:
                    for key in keys:
                        tile[tk, key] = tile[tk, key] - below * rows[q, key]
                for p in range(q + 1, 8):
                    coef = jnp.broadcast_to(cols[tk, p][q:q + 1, :], (8, 128)) * recip
                    cols[tk, p] = cols[tk, p] - below * coef
                    for t in range(tk + 1, nt):
                        cols[t, p] = cols[t, p] - cols[t, q] * coef
            for t in range(tk + 1, nt):
                for key in keys:
                    acc = tile[t, key]
                    for q in range(8):
                        acc = acc - cols[t, q] * rows[q, key]
                    tile[t, key] = acc
        for t in range(nt):
            at = sub + (r0 + t * 8 - first * 128)
            diag = jnp.sum(jnp.where(lane == at, tile[t, pk], 0.0), axis=1, keepdims=True)
            scale_rows = jnp.broadcast_to(1.0 / jnp.sqrt(diag), (8, 128))
            for key in keys:
                value = tile[t, key] * scale_rows
                if key == pk:
                    value = jnp.where(lane >= at, value, 0.0)
                (r_ref if key[0] == "r" else l_ref)[r0 + t * 8:r0 + t * 8 + 8, key[1] * 128:(key[1] + 1) * 128] = value
    sf_ref[...] = r_ref[...] * scale
    high, mid, low = thirds(l_ref[...].T)
    for at, part in enumerate([high, mid, low, high, mid, high]):
        inv_ref[at * n:(at + 1) * n, :] = part

def factorize(gram, scale):
    size = gram.shape[0]
    return pl.pallas_call(
        functools.partial(factor_kernel, scale),
        out_shape=[
            jax.ShapeDtypeStruct((size, size), jnp.float32),
            jax.ShapeDtypeStruct((6 * size, size), jnp.bfloat16),
        ],
        in_specs=[pl.BlockSpec(memory_space=pltpu.VMEM)],
        out_specs=[pl.BlockSpec(memory_space=pltpu.VMEM)] * 2,
        scratch_shapes=[pltpu.VMEM((size, size), jnp.float32)] * 2,
        cost_estimate=LIGHT,
        name="factorize",
    )(gram)


def basis_of(value, inverse):
    high, mid, low = thirds(value)
    terms = jnp.concatenate([low, mid, high, mid, high, high], axis=1)
    return jnp.dot(terms, inverse, preferred_element_type=jnp.float32)


def turn(basis, turned_ref):
    turned = basis.T
    high = turned.astype(jnp.bfloat16)
    rest = (turned - high.astype(jnp.float32)).astype(jnp.bfloat16)
    size = turned_ref.shape[2] // 2
    for i in range(turned_ref.shape[0]):
        span = slice(i * size, (i + 1) * size)
        turned_ref[i] = jnp.concatenate([high[:, span], rest[:, span]], axis=1)


def late_basis_kernel(x_ref, inv_ref, send_ref, half_ref, turned_ref):
    basis = basis_of(x_ref[...], inv_ref[...])
    half = basis.astype(jnp.bfloat16)
    send_ref[...] = half
    half_ref[...] = half
    turn(basis, turned_ref)


def late_basis(snapshots, inverse, start, size):
    rows, width = snapshots.shape
    tile = math.gcd(math.gcd(start, rows), ROW_TILE)
    first = start // tile
    shifted = pl.BlockSpec((tile, width), lambda i: (i + first, 0))
    return pl.pallas_call(
        late_basis_kernel,
        grid=((rows - start) // tile,),
        in_specs=[shifted, pl.BlockSpec(inverse.shape, lambda i: (0, 0))],
        out_specs=[
            pl.BlockSpec((tile, width), lambda i: (i, 0)),
            shifted,
            pl.BlockSpec((tile // size, width, 2 * size), lambda i: (i + first, 0, 0)),
        ],
        out_shape=[
            jax.ShapeDtypeStruct((rows - start, width), jnp.bfloat16),
            jax.ShapeDtypeStruct((rows, width), jnp.bfloat16),
            jax.ShapeDtypeStruct((rows // size, width, 2 * size), jnp.bfloat16),
        ],
        compiler_params=pltpu.CompilerParams(vmem_limit_bytes=EARLY_VMEM),
        cost_estimate=LIGHT,
        name="late_basis",
    )(snapshots, inverse)


def early_basis_kernel(ends, x_ref, one_ref, two_ref, inv_ref, _, __, half_ref, turned_ref, other_ref):
    step = pl.program_id(0)
    value = jnp.where(step < ends[0], x_ref[...], jnp.where(step < ends[1], one_ref[...], two_ref[...]))
    basis = basis_of(value, inv_ref[...])

    @pl.when(step < ends[0])
    def _():
        half_ref[...] = basis.astype(jnp.bfloat16)
        turn(basis, turned_ref)

    @pl.when(step >= ends[0])
    def _():
        other_ref[...] = basis.astype(jnp.bfloat16)


def early_basis(snapshots, one, two, inverse, half, turned):
    width = snapshots.shape[1]
    tile = math.gcd(math.gcd(one.shape[0], two.shape[0]), ROW_TILE)
    own = (one.shape[0] + two.shape[0]) // tile
    mid = own + one.shape[0] // tile
    spec = lambda index: pl.BlockSpec((tile, width), index)
    here = lambda i: jnp.minimum(i, own - 1)
    return pl.pallas_call(
        functools.partial(early_basis_kernel, (own, mid)),
        grid=(2 * own,),
        in_specs=[
            spec(lambda i: (here(i), 0)),
            spec(lambda i: (jnp.clip(i - own, 0, mid - own - 1), 0)),
            spec(lambda i: (jnp.maximum(i - mid, 0), 0)),
            pl.BlockSpec(inverse.shape, lambda i: (0, 0)),
            pl.BlockSpec(memory_space=pl.ANY),
            pl.BlockSpec(memory_space=pl.ANY),
        ],
        out_specs=[
            spec(lambda i: (here(i), 0)),
            pl.BlockSpec((tile * turned.shape[0] // snapshots.shape[0],) + turned.shape[1:], lambda i: (here(i), 0, 0)),
            spec(lambda i: (jnp.maximum(i - own, 0), 0)),
        ],
        out_shape=[
            jax.ShapeDtypeStruct(half.shape, half.dtype),
            jax.ShapeDtypeStruct(turned.shape, turned.dtype),
            jax.ShapeDtypeStruct((own * tile, width), half.dtype),
        ],
        input_output_aliases={4: 0, 5: 1},
        compiler_params=pltpu.CompilerParams(vmem_limit_bytes=EARLY_VMEM),
        cost_estimate=LIGHT,
        name="early_basis",
    )(snapshots, one, two, inverse, half, turned)


def split_pair(value):
    high = value.astype(jnp.bfloat16)
    rest = (value - high.astype(jnp.float32)).astype(jnp.bfloat16)
    return jnp.concatenate([high, rest], axis=1)


def doubled(half):
    return jnp.concatenate([half, half], axis=0)


def early_kernel(places, spot_ref, blocks_ref, turned_ref, *refs):
    pieces, (out_ref, left_ref, sums_ref, window_ref, sems) = refs[:-5], refs[-5:]
    step = pl.program_id(0)
    size = blocks_ref.shape[2]
    copies = [
        pltpu.make_async_copy(piece, window_ref.at[pl.ds(at, piece.shape[0])], sems.at[i])
        for i, (piece, at) in enumerate(zip(pieces, places))
    ]

    @pl.when(step == 0)
    def _():
        for copy in copies:
            copy.start()
        sums_ref[...] = jnp.zeros_like(sums_ref)

    for row in range(PAIR):
        at = step * PAIR + row
        for j in range(0, blocks_ref.shape[1], 2):
            pair = jnp.concatenate([blocks_ref[row, j], blocks_ref[row, j + 1]], axis=1)
            term = jnp.dot(turned_ref[row], doubled(pair), preferred_element_type=jnp.float32)
            sums_ref[spot_ref[at, j]] += term[:, :size]
            sums_ref[spot_ref[at, j + 1]] += term[:, size:]

    @pl.when(step == pl.num_programs(0) - 1)
    def _():
        for copy in copies:
            copy.wait()
        known = window_ref.shape[0]
        total = jnp.zeros_like(out_ref)
        for c in range(known):
            total += jnp.dot(
                split_pair(sums_ref[c]), doubled(window_ref[c]), preferred_element_type=jnp.float32
            )
        out_ref[...] = total
        for c in range(left_ref.shape[0]):
            left_ref[c] = split_pair(sums_ref[known + c])


def early_terms(spots, blocks, turned, pieces, slots):
    count, stored, size, _ = blocks.shape
    width = turned.shape[1]
    pieces = [piece.reshape(piece.shape[0] // size, size, width) for piece in pieces]
    places = [sum(piece.shape[0] for piece in pieces[:i]) for i in range(len(pieces))]
    known = places[-1] + pieces[-1].shape[0]
    return pl.pallas_call(
        functools.partial(early_kernel, places),
        grid_spec=pltpu.PrefetchScalarGridSpec(
            num_scalar_prefetch=1,
            grid=(count // PAIR,),
            in_specs=[
                pl.BlockSpec((PAIR, stored, size, size), lambda i, *_: (i, 0, 0, 0)),
                pl.BlockSpec((PAIR, width, 2 * size), lambda i, *_: (i, 0, 0)),
            ]
            + [pl.BlockSpec(memory_space=pl.ANY)] * len(pieces),
            out_specs=[
                pl.BlockSpec((width, width), lambda i, *_: (0, 0)),
                pl.BlockSpec((slots - known, width, 2 * size), lambda i, *_: (0, 0, 0)),
            ],
            scratch_shapes=[
                pltpu.VMEM((slots, width, size), jnp.float32),
                pltpu.VMEM((known, size, width), jnp.bfloat16),
                pltpu.SemaphoreType.DMA((len(pieces),)),
            ],
        ),
        out_shape=[
            jax.ShapeDtypeStruct((width, width), jnp.float32),
            jax.ShapeDtypeStruct((slots - known, width, 2 * size), jnp.bfloat16),
        ],
        compiler_params=pltpu.CompilerParams(vmem_limit_bytes=EARLY_VMEM),
        cost_estimate=LIGHT,
        name="early_terms",
    )(spots, blocks, turned, *pieces)


def late_kernel(early_ref, left_ref, half_ref, out_ref):
    @pl.when(pl.program_id(0) == 0)
    def _():
        out_ref[...] = early_ref[...]

    total = out_ref[...]
    for c in range(left_ref.shape[0]):
        total += jnp.dot(left_ref[c], doubled(half_ref[c]), preferred_element_type=jnp.float32)
    out_ref[...] = total


def late_terms(early, left, half):
    slots, width, size = left.shape[0], left.shape[1], left.shape[2] // 2
    step = slots // LATE_STEPS
    return pl.pallas_call(
        late_kernel,
        grid=(LATE_STEPS,),
        in_specs=[
            pl.BlockSpec((width, width), lambda i: (0, 0)),
            pl.BlockSpec((step, width, 2 * size), lambda i: (i, 0, 0)),
            pl.BlockSpec((step, size, width), lambda i: (i, 0, 0)),
        ],
        out_specs=pl.BlockSpec((width, width), lambda i: (0, 0)),
        out_shape=jax.ShapeDtypeStruct(early.shape, jnp.float32),
        compiler_params=pltpu.CompilerParams(vmem_limit_bytes=EARLY_VMEM),
        cost_estimate=LIGHT,
        name="late_terms",
    )(early, left, half.reshape(slots, size, width))


def spread(value, axes):
    devices = lax.axis_size(axes)
    rows, width = value.shape
    copies = jnp.broadcast_to(value[None], (devices, rows, width))
    return lax.all_to_all(copies, axes, 0, 0, tiled=True).reshape(devices * rows, width)


def reduce_share(value, axes):
    devices = lax.axis_size(axes)
    rows, width = value.shape
    parts = lax.all_to_all(value.reshape(devices, rows // devices, width), axes, 0, 0, tiled=True)
    return parts.sum(axis=0)


def total(value):
    return spread(reduce_share(value, AXES), AXES)


def exchange(value, axes, mask):
    return lax.ppermute(value, axes, [(i, i ^ mask) for i in range(lax.axis_size(axes))])


def local(snapshots, blocks, columns):
    rows = snapshots.shape[0]
    size = blocks.shape[2]
    count = rows // size
    first, raw = FIRST * size, RAW * size
    partner_first = exchange(snapshots[:first], "yl", 1)
    gram, following = local_gram(snapshots, first, raw)
    share = reduce_share(gram, SIDE)
    share, partner_first = lax.optimization_barrier((share, partner_first))
    near = [exchange(share, ("yh", "yl"), mask) for mask in (1, 2, 3)]
    share = (share + near[0]) + (near[1] + near[2])
    share, following = lax.optimization_barrier((share, following))
    partner_second = exchange(following, "yl", 1)
    gram = spread(share, SIDE)
    total_rows = rows * lax.axis_size(AXES)
    scaled_factor, inverse = factorize(gram, 1.0 / math.sqrt(total_rows))
    late_half, half, turned = late_basis(snapshots, inverse, raw, size)
    partner_late = exchange(late_half, "yl", 1)
    half, turned, other_half = early_basis(snapshots, partner_first, partner_second, inverse, half, turned)
    own = columns // count == lax.axis_index("yl")
    spots = columns % count + jnp.where(own, 0, count)
    early, left = early_terms(spots, blocks, turned, [half, other_half], 2 * count)
    projected = total(late_terms(early, left, partner_late))
    return (projected, scaled_factor)


def solution(mesh):
    sizes = (4, 2, 4, 2, 2)
    fine = jax.sharding.Mesh(mesh.devices.reshape(sizes), AXES)
    return jax.shard_map(
        local,
        mesh=fine,
        in_specs=(
            P(AXES, None),
            P(AXES, None, None, None),
            P(AXES, None),
        ),
        out_specs=(P(), P()),
        check_vma=False,
    )
```

```python
import functools
import math

import jax
import jax.numpy as jnp
from jax import lax
from jax.experimental import pallas as pl
from jax.experimental.pallas import tpu as pltpu
from jax.sharding import PartitionSpec as P

HIGHEST = lax.Precision.HIGHEST
AXES = ("x", "yh", "z", "core", "yl")
SIDE = ("x", "z", "core")
PANEL = 64
FIRST = 4
RAW = 12
GRAM_TILE = 2048
ROW_TILE = 1024
PAIR = 8
LIGHT = pl.CostEstimate(flops=0, transcendentals=0, bytes_accessed=0)
EARLY_VMEM = 56 << 20


def tdot(left, right):
    return lax.dot_general(left, right, (((0,), (0,)), ((), ())), preferred_element_type=jnp.float32)


def thirds(value):
    high = value.astype(jnp.bfloat16)
    rest = value - high.astype(jnp.float32)
    mid = rest.astype(jnp.bfloat16)
    low = (rest - mid.astype(jnp.float32)).astype(jnp.bfloat16)
    return high, mid, low


def gram_kernel(x_ref, g_ref, lead_ref, sym_ref, off_ref):
    step = pl.program_id(0)

    @pl.when(step == 0)
    def _():
        lead_ref[...] = x_ref[:lead_ref.shape[0], :]

    @pl.when(step == 0)
    def _():
        sym_ref[...] = jnp.zeros_like(sym_ref)
        off_ref[...] = jnp.zeros_like(off_ref)

    high, mid, low = thirds(x_ref[...])
    both = jnp.concatenate([high, mid], axis=0)
    sym_ref[...] += tdot(both, both)
    off_ref[...] += tdot(jnp.concatenate([high, high], axis=0), jnp.concatenate([mid, low], axis=0))

    @pl.when(step == pl.num_programs(0) - 1)
    def _():
        off = off_ref[...]
        g_ref[...] = sym_ref[...] + (off + off.T)


def local_gram(snapshots, first):
    rows, width = snapshots.shape
    shapes = [(width, width), (first, width)]
    return pl.pallas_call(
        gram_kernel,
        grid=(rows // GRAM_TILE,),
        in_specs=[pl.BlockSpec((GRAM_TILE, width), lambda i: (i, 0))],
        out_specs=[pl.BlockSpec(shape, lambda i: (0, 0)) for shape in shapes],
        out_shape=[jax.ShapeDtypeStruct(shape, jnp.float32) for shape in shapes],
        scratch_shapes=[pltpu.VMEM((width, width), jnp.float32)] * 2,
        cost_estimate=LIGHT,
        name="local_gram",
    )(snapshots)


def factor_kernel(scale, g_ref, sf_ref, inv_ref, r_ref, l_ref):
    n = g_ref.shape[0]
    sub = lax.broadcasted_iota(jnp.int32, (8, 128), 0)
    lane = lax.broadcasted_iota(jnp.int32, (8, 128), 1)
    r_ref[...] = jnp.zeros_like(r_ref)
    l_ref[...] = jnp.zeros_like(l_ref)
    for r0 in range(0, n, PANEL):
        first = r0 // 128
        keys = [("r", i) for i in range(first, n // 128)] + [("l", i) for i in range(first + 1)]
        depth = -(-r0 // 128) * 128
        left = None
        if depth:
            a = first * 128
            left = r_ref[0:depth, a:a + 128].T[r0 - a:r0 - a + PANEL, :]
        tile = {}
        for key in keys:
            kind, i = key
            if kind == "r":
                part = g_ref[r0:r0 + PANEL, i * 128:(i + 1) * 128]
            else:
                rows = lax.broadcasted_iota(jnp.int32, (PANEL, 128), 0) + r0
                cols = lax.broadcasted_iota(jnp.int32, (PANEL, 128), 1) + i * 128
                part = jnp.where(rows == cols, 1.0, 0.0).astype(jnp.float32)
            if depth:
                right = (r_ref if kind == "r" else l_ref)[0:depth, i * 128:(i + 1) * 128]
                part = part - jnp.dot(left, right, precision=HIGHEST, preferred_element_type=jnp.float32)
            for t in range(PANEL // 8):
                tile[t, key] = part[t * 8:(t + 1) * 8, :]
        pk = ("r", first)
        nt = PANEL // 8
        for tk in range(nt):
            c0 = (r0 + tk * 8) % 128
            cols = {}
            for q in range(8):
                for t in range(tk, nt):
                    cols[t, q] = jnp.broadcast_to(tile[t, pk][:, c0 + q:c0 + q + 1], (8, 128))
            rows = {}
            for q in range(8):
                pivot = jnp.broadcast_to(cols[tk, q][q:q + 1, :], (8, 128))
                recip = 1.0 / pivot
                for key in keys:
                    rows[q, key] = jnp.broadcast_to(tile[tk, key][q:q + 1, :], (8, 128)) * recip
                below = jnp.where(sub > q, cols[tk, q], 0.0)
                if q < 7:
                    for key in keys:
                        tile[tk, key] = tile[tk, key] - below * rows[q, key]
                for p in range(q + 1, 8):
                    coef = jnp.broadcast_to(cols[tk, p][q:q + 1, :], (8, 128)) * recip
                    cols[tk, p] = cols[tk, p] - below * coef
                    for t in range(tk + 1, nt):
                        cols[t, p] = cols[t, p] - cols[t, q] * coef
            for t in range(tk + 1, nt):
                for key in keys:
                    acc = tile[t, key]
                    for q in range(8):
                        acc = acc - cols[t, q] * rows[q, key]
                    tile[t, key] = acc
        for t in range(nt):
            at = sub + (r0 + t * 8 - first * 128)
            diag = jnp.sum(jnp.where(lane == at, tile[t, pk], 0.0), axis=1, keepdims=True)
            scale_rows = jnp.broadcast_to(1.0 / jnp.sqrt(diag), (8, 128))
            for key in keys:
                value = tile[t, key] * scale_rows
                if key == pk:
                    value = jnp.where(lane >= at, value, 0.0)
                (r_ref if key[0] == "r" else l_ref)[r0 + t * 8:r0 + t * 8 + 8, key[1] * 128:(key[1] + 1) * 128] = value
    sf_ref[...] = r_ref[...] * scale
    high, mid, low = thirds(l_ref[...].T)
    for at, part in enumerate([high, mid, low, high, mid, high]):
        inv_ref[at * n:(at + 1) * n, :] = part

def factorize(gram, scale):
    size = gram.shape[0]
    return pl.pallas_call(
        functools.partial(factor_kernel, scale),
        out_shape=[
            jax.ShapeDtypeStruct((size, size), jnp.float32),
            jax.ShapeDtypeStruct((6 * size, size), jnp.bfloat16),
        ],
        in_specs=[pl.BlockSpec(memory_space=pltpu.VMEM)],
        out_specs=[pl.BlockSpec(memory_space=pltpu.VMEM)] * 2,
        scratch_shapes=[pltpu.VMEM((size, size), jnp.float32)] * 2,
        cost_estimate=LIGHT,
        name="factorize",
    )(gram)


def basis_of(value, inverse):
    high, mid, low = thirds(value)
    terms = jnp.concatenate([low, mid, high, mid, high, high], axis=1)
    return jnp.dot(terms, inverse, preferred_element_type=jnp.float32)


def own_basis_kernel(x_ref, inv_ref, *refs):
    half_ref, turned_ref = refs[-2:]
    basis = basis_of(x_ref[...], inv_ref[...])
    half = basis.astype(jnp.bfloat16)
    half_ref[...] = half
    if len(refs) == 3:
        refs[0][...] = half
    turned = basis.T
    high = turned.astype(jnp.bfloat16)
    rest = (turned - high.astype(jnp.float32)).astype(jnp.bfloat16)
    size = turned_ref.shape[2] // 2
    for i in range(turned_ref.shape[0]):
        span = slice(i * size, (i + 1) * size)
        turned_ref[i] = jnp.concatenate([high[:, span], rest[:, span]], axis=1)


def own_basis(snapshots, inverse, start, stop, size, held=None):
    rows, width = snapshots.shape
    tile = math.gcd(math.gcd(start, stop), ROW_TILE)
    first = start // tile
    shifted = pl.BlockSpec((tile, width), lambda i: (i + first, 0))
    half = jax.ShapeDtypeStruct((rows, width), jnp.bfloat16)
    turned = jax.ShapeDtypeStruct((rows // size, width, 2 * size), jnp.bfloat16)
    out_specs = [shifted, pl.BlockSpec((tile // size, width, 2 * size), lambda i: (i + first, 0, 0))]
    out_shape = [half, turned]
    if held is None:
        out_specs = [pl.BlockSpec((tile, width), lambda i: (i, 0))] + out_specs
        out_shape = [jax.ShapeDtypeStruct((stop - start, width), jnp.bfloat16)] + out_shape
    held = held or []
    return pl.pallas_call(
        own_basis_kernel,
        grid=((stop - start) // tile,),
        in_specs=[shifted, pl.BlockSpec(inverse.shape, lambda i: (0, 0))]
        + [pl.BlockSpec(memory_space=pl.ANY)] * len(held),
        out_specs=out_specs,
        out_shape=out_shape,
        input_output_aliases={2 + i: i for i in range(len(held))},
        cost_estimate=LIGHT,
        name="own_basis",
    )(snapshots, inverse, *held)


def other_basis_kernel(switch, one_ref, two_ref, inv_ref, out_ref):
    value = jnp.where(pl.program_id(0) < switch, one_ref[...], two_ref[...])
    out_ref[...] = basis_of(value, inv_ref[...]).astype(jnp.bfloat16)


def other_basis(one, two, inverse):
    width = one.shape[1]
    tile = math.gcd(math.gcd(one.shape[0], two.shape[0]), ROW_TILE)
    switch, steps = one.shape[0] // tile, (one.shape[0] + two.shape[0]) // tile
    return pl.pallas_call(
        functools.partial(other_basis_kernel, switch),
        grid=(steps,),
        in_specs=[
            pl.BlockSpec((tile, width), lambda i: (jnp.minimum(i, switch - 1), 0)),
            pl.BlockSpec((tile, width), lambda i: (jnp.maximum(i - switch, 0), 0)),
            pl.BlockSpec(inverse.shape, lambda i: (0, 0)),
        ],
        out_specs=pl.BlockSpec((tile, width), lambda i: (i, 0)),
        out_shape=jax.ShapeDtypeStruct((steps * tile, width), jnp.bfloat16),
        cost_estimate=LIGHT,
        name="other_basis",
    )(one, two, inverse)


def split_pair(value):
    high = value.astype(jnp.bfloat16)
    rest = (value - high.astype(jnp.float32)).astype(jnp.bfloat16)
    return jnp.concatenate([high, rest], axis=1)


def doubled(half):
    return jnp.concatenate([half, half], axis=0)


def early_kernel(places, spot_ref, blocks_ref, turned_ref, *refs):
    pieces, (out_ref, left_ref, sums_ref, window_ref, sems) = refs[:-5], refs[-5:]
    step = pl.program_id(0)
    size = blocks_ref.shape[2]
    copies = [
        pltpu.make_async_copy(piece, window_ref.at[pl.ds(at, piece.shape[0])], sems.at[i])
        for i, (piece, at) in enumerate(zip(pieces, places))
    ]

    @pl.when(step == 0)
    def _():
        for copy in copies:
            copy.start()
        sums_ref[...] = jnp.zeros_like(sums_ref)

    for row in range(PAIR):
        at = step * PAIR + row
        for j in range(0, blocks_ref.shape[1], 2):
            pair = jnp.concatenate([blocks_ref[row, j], blocks_ref[row, j + 1]], axis=1)
            term = jnp.dot(turned_ref[row], doubled(pair), preferred_element_type=jnp.float32)
            sums_ref[spot_ref[at, j]] += term[:, :size]
            sums_ref[spot_ref[at, j + 1]] += term[:, size:]

    @pl.when(step == pl.num_programs(0) - 1)
    def _():
        for copy in copies:
            copy.wait()
        known = window_ref.shape[0]
        total = jnp.zeros_like(out_ref)
        for c in range(known):
            total += jnp.dot(
                split_pair(sums_ref[c]), doubled(window_ref[c]), preferred_element_type=jnp.float32
            )
        out_ref[...] = total
        for c in range(left_ref.shape[0]):
            left_ref[c] = split_pair(sums_ref[known + c])


def early_terms(spots, blocks, turned, pieces, slots):
    count, stored, size, _ = blocks.shape
    width = turned.shape[1]
    pieces = [piece.reshape(piece.shape[0] // size, size, width) for piece in pieces]
    places = [sum(piece.shape[0] for piece in pieces[:i]) for i in range(len(pieces))]
    known = places[-1] + pieces[-1].shape[0]
    return pl.pallas_call(
        functools.partial(early_kernel, places),
        grid_spec=pltpu.PrefetchScalarGridSpec(
            num_scalar_prefetch=1,
            grid=(count // PAIR,),
            in_specs=[
                pl.BlockSpec((PAIR, stored, size, size), lambda i, *_: (i, 0, 0, 0)),
                pl.BlockSpec((PAIR, width, 2 * size), lambda i, *_: (i, 0, 0)),
            ]
            + [pl.BlockSpec(memory_space=pl.ANY)] * len(pieces),
            out_specs=[
                pl.BlockSpec((width, width), lambda i, *_: (0, 0)),
                pl.BlockSpec((slots - known, width, 2 * size), lambda i, *_: (0, 0, 0)),
            ],
            scratch_shapes=[
                pltpu.VMEM((slots, width, size), jnp.float32),
                pltpu.VMEM((known, size, width), jnp.bfloat16),
                pltpu.SemaphoreType.DMA((len(pieces),)),
            ],
        ),
        out_shape=[
            jax.ShapeDtypeStruct((width, width), jnp.float32),
            jax.ShapeDtypeStruct((slots - known, width, 2 * size), jnp.bfloat16),
        ],
        compiler_params=pltpu.CompilerParams(vmem_limit_bytes=EARLY_VMEM),
        cost_estimate=LIGHT,
        name="early_terms",
    )(spots, blocks, turned, *pieces)


def late_kernel(early_ref, left_ref, half_ref, out_ref):
    total = early_ref[...]
    for c in range(left_ref.shape[0]):
        total += jnp.dot(left_ref[c], doubled(half_ref[c]), preferred_element_type=jnp.float32)
    out_ref[...] = total


def late_terms(early, left, half):
    size = left.shape[2] // 2
    return pl.pallas_call(
        late_kernel,
        in_specs=[pl.BlockSpec(memory_space=pltpu.VMEM)] * 3,
        out_specs=pl.BlockSpec(memory_space=pltpu.VMEM),
        out_shape=jax.ShapeDtypeStruct(early.shape, jnp.float32),
        cost_estimate=LIGHT,
        name="late_terms",
    )(early, left, half.reshape(left.shape[0], size, half.shape[1]))


def spread(value, axes):
    devices = lax.axis_size(axes)
    rows, width = value.shape
    copies = jnp.broadcast_to(value[None], (devices, rows, width))
    return lax.all_to_all(copies, axes, 0, 0, tiled=True).reshape(devices * rows, width)


def reduce_share(value, axes):
    devices = lax.axis_size(axes)
    rows, width = value.shape
    parts = lax.all_to_all(value.reshape(devices, rows // devices, width), axes, 0, 0, tiled=True)
    return parts.sum(axis=0)


def total(value):
    return spread(reduce_share(value, AXES), AXES)


def exchange(value, axes, mask):
    return lax.ppermute(value, axes, [(i, i ^ mask) for i in range(lax.axis_size(axes))])


def local(snapshots, blocks, columns):
    rows = snapshots.shape[0]
    size = blocks.shape[2]
    count = rows // size
    first, raw = FIRST * size, RAW * size
    gram, leading = local_gram(snapshots, first)
    partner_first = exchange(leading, "yl", 1)
    share = reduce_share(gram, SIDE)
    share, partner_first = lax.optimization_barrier((share, partner_first))
    near = [exchange(share, ("yh", "yl"), mask) for mask in (1, 2, 3)]
    share = (share + near[0]) + (near[1] + near[2])
    share, following = lax.optimization_barrier((share, snapshots[first:raw]))
    partner_second = exchange(following, "yl", 1)
    gram = spread(share, SIDE)
    total_rows = rows * lax.axis_size(AXES)
    scaled_factor, inverse = factorize(gram, 1.0 / math.sqrt(total_rows))
    late_half, half, turned = own_basis(snapshots, inverse, raw, rows, size)
    late_half, partner_second = lax.optimization_barrier((late_half, partner_second))
    partner_late = exchange(late_half, "yl", 1)
    half, turned = own_basis(snapshots, inverse, 0, raw, size, [half, turned])
    other_half = other_basis(partner_first, partner_second, inverse)
    own = columns // count == lax.axis_index("yl")
    spots = columns % count + jnp.where(own, 0, count)
    early, left = early_terms(spots, blocks, turned, [half, other_half], 2 * count)
    projected = total(late_terms(early, left, partner_late))
    return (projected, scaled_factor)


def solution(mesh):
    sizes = (4, 2, 4, 2, 2)
    fine = jax.sharding.Mesh(mesh.devices.reshape(sizes), AXES)
    return jax.shard_map(
        local,
        mesh=fine,
        in_specs=(
            P(AXES, None),
            P(AXES, None, None, None),
            P(AXES, None),
        ),
        out_specs=(P(), P()),
        check_vma=False,
    )
```
